1024 devices in a mesh: row: 8 (over z_lo), col: 128 (over x, z_hi, y, core).
Axes of the slice: x: 4, y: 8, z: 16 (z_hi: 2, z_lo: 8; z = z_hi * 8 + z_lo), core: 2. Of those that a mesh axis runs over, the one named last changes fastest.
Arguments:
- trailing: bfloat16 [8192, 65536], P('row', 'col'), may hold values from -12 to 12
- panel_left: bfloat16 [8192, 1024], P(('row', 'col')), may hold values from -1.5 to 1.5
- panel_right: bfloat16 [65536, 1024], P(('col', 'row')), may hold values from -1.5 to 1.5
- inverse_factors: float32 [2, 512, 512], replicated, may hold values from -2 to 2, as said below
- active: int32 [16, 128], P('row', 'col'), may hold values 0 or 1
Outputs:
- updated: bfloat16 [8192, 65536], P('row', 'col')
The draws below stay inside these ranges and needn't reach their ends.
Inputs may be any that keep to these rules, and one draw needn't show every extreme that they name: `inverse_factors`: lower triangular, positive diagonal.
All inputs are finite; a program needn't handle non-finite values. No bound on the sum of `active` on one device may be relied on, other than what follows from the above.
Results may differ from the reference program's by a relative error of at most 0.0052.
Values may be sent and summed in bfloat16 or wider, within the bound.
No kernel may reach another device: no remote copies, remote signals or barrier semaphores. Data moves between devices by JAX's collectives and lax.ppermute only.
A program may use at most 32 MiB of HBM per device.

```python
import jax
import jax.numpy as jnp
from jax import lax

TILE = 512
PANELS = 2
MT = 16
NT = 128
ROWS = 8192
COLS = 65536


def draw_inverse_factors(key, part):
    first, second = jax.random.split(jax.random.fold_in(key, 71))
    diag_vals = jnp.exp(jax.random.uniform(first, (PANELS, TILE), jnp.float32, jnp.log(0.5), jnp.log(2.0)))
    lower = jax.random.normal(second, (PANELS, TILE, TILE), jnp.float32) * (0.5 / TILE ** 0.5)
    strict = jnp.tril(lower, -1)
    eye_mat = jnp.eye(TILE, dtype=jnp.float32)
    return strict + eye_mat[None, :, :] * diag_vals[:, None, :]


def with_ends(drawn, stream_key, least, high):
    place = [jax.random.randint(jax.random.fold_in(stream_key, axis), (), 0, length) for axis, length in enumerate(drawn.shape)]
    main_axis = drawn.shape.index(max(drawn.shape))
    beside = place[:main_axis] + [(place[main_axis] + 1) % drawn.shape[main_axis]] + place[main_axis + 1:]
    return drawn.at[tuple(place)].set(least).at[tuple(beside)].set(high)


def level_of(own_key, extent, cuts, smallest, largest):
    gain = 1.0
    for axis_at, blocks in cuts:
        heights = jax.random.uniform(jax.random.fold_in(jax.random.fold_in(own_key, 6), axis_at), (blocks,), jnp.float32, smallest / len(cuts), largest / len(cuts))
        gain = gain * jnp.repeat(jnp.exp(heights), extent[axis_at] // blocks).reshape((-1,) + (1,) * (len(extent) - 1 - axis_at))
    return gain


def centred(stream_key, extent, scale, reach, cuts=(), kind=jnp.bfloat16):
    drawn = jax.random.normal(stream_key, extent, jnp.float32) * scale
    if len(cuts) > 0:
        drawn = level_of(stream_key, extent, cuts, -0.22, 0.18) * drawn
    return jnp.clip(drawn, min=-reach, max=reach).astype(kind)


def setup_inputs(seed: int = 0) -> dict:
    splits = jax.random.split(jax.random.key(seed), 6)
    return {
        "trailing": centred(splits[0], (ROWS, COLS), 2.0, 12.0, ((0, 8), (1, 128))),
        "panel_left": centred(splits[1], (ROWS, PANELS * TILE), 0.25, 1.5, ((0, 1024),)),
        "panel_right": centred(splits[2], (COLS, PANELS * TILE), 0.25, 1.5, ((0, 1024),)),
        "inverse_factors": draw_inverse_factors(jax.random.fold_in(splits[5], 71), 0),
        "active": with_ends((jax.random.randint(splits[4], (MT, NT), 0, 5) < 3).astype(jnp.int32), jax.random.fold_in(splits[4], 1), 0, 1),
    }


def triangle(rows, inverse_factors):
    width = inverse_factors.shape[1]
    parts = []
    for panel in range(inverse_factors.shape[0]):
        block = rows[:, panel * width:(panel + 1) * width].astype(jnp.float32)
        parts.append(jnp.dot(block, inverse_factors[panel].T, precision=lax.Precision.HIGHEST, preferred_element_type=jnp.float32))
    return jnp.concatenate(parts, axis=1).astype(jnp.bfloat16)


def reference(trailing, panel_left, panel_right, inverse_factors, active):
    factor_left = triangle(panel_left, inverse_factors)
    factor_right = triangle(panel_right, inverse_factors)
    width = inverse_factors.shape[1]
    right_tiles = factor_right.reshape(NT, width, factor_right.shape[1])
    trail_tiles = jnp.transpose(trailing.reshape(ROWS, NT, width), (1, 0, 2))
    mask_cols = jnp.transpose(active, (1, 0))

    def one_column(items):
        right_tile, trail_tile, mask_col = items
        change = lax.dot_general(factor_left, right_tile, (((1,), (1,)), ((), ())), preferred_element_type=jnp.float32)
        keep = jnp.repeat(mask_col, width)[:, None] == 1
        fresh = trail_tile.astype(jnp.float32) - change
        return jnp.where(keep, fresh, trail_tile.astype(jnp.float32)).astype(jnp.bfloat16)

    columns = lax.map(one_column, (right_tiles, trail_tiles, mask_cols))
    return jnp.transpose(columns, (1, 0, 2)).reshape(ROWS, COLS)
```

```python
import functools

import jax
import jax.numpy as jnp
from jax import lax
from jax.experimental import pallas as pl
from jax.experimental.pallas import tpu as pltpu
from jax.sharding import Mesh, PartitionSpec as P


VMEM = pl.BlockSpec(memory_space=pltpu.VMEM)
SMEM = pl.BlockSpec(memory_space=pltpu.SMEM)
SMALL = pltpu.CompilerParams(vmem_limit_bytes=16 * 2**20)


def factor_rows(rows, inverse_ref, store):
    panels, width, _ = inverse_ref.shape
    half = width // 2
    for panel in range(panels):
        for at in range(2):
            depth = (at + 1) * half
            block = rows[:, panel * width : panel * width + depth]
            exact = inverse_ref[panel, at * half : (at + 1) * half, :depth]
            high = exact.astype(jnp.bfloat16)
            rest = exact - high.astype(jnp.float32)
            middle = rest.astype(jnp.bfloat16)
            low = (rest - middle.astype(jnp.float32)).astype(jnp.bfloat16)
            total = None
            for part in (low, middle, high):
                term = lax.dot_general(
                    block, part, (((1,), (1,)), ((), ())), preferred_element_type=jnp.float32
                )
                total = term if total is None else total + term
            store(panel * width + at * half, total.astype(jnp.bfloat16))


def right_kernel(first_ref, second_ref, inverse_ref, out_ref):
    half = inverse_ref.shape[1] // 2

    def store(start, values):
        out_ref[:, start : start + half] = values

    rows = jnp.concatenate([first_ref[...], second_ref[...]], axis=0)
    factor_rows(rows, inverse_ref, store)


def left_kernel(core_ref, near_ref, inverse_ref, out_ref):
    half = inverse_ref.shape[1] // 2

    def store(start, values):
        out_ref[:, start : start + half] = values

    factor_rows(near_ref[core_ref[0]], inverse_ref, store)


def factor_cost(count, inverse):
    return pl.CostEstimate(
        flops=6 * count * inverse.shape[0] * inverse.shape[1] ** 2,
        bytes_accessed=inverse.size * 4 + 4 * count * inverse.shape[0] * inverse.shape[1],
        transcendentals=0,
    )


def factor_right(first, second, inverse):
    count = 2 * first.shape[0]
    return pl.pallas_call(
        right_kernel,
        out_shape=jax.ShapeDtypeStruct((count, first.shape[1]), jnp.bfloat16),
        in_specs=[VMEM, VMEM, VMEM],
        out_specs=VMEM,
        cost_estimate=factor_cost(count, inverse),
        compiler_params=SMALL,
        name="factor_right",
    )(first, second, inverse)


def factor_left(core, near, inverse):
    count = near.shape[1]
    return pl.pallas_call(
        left_kernel,
        out_shape=jax.ShapeDtypeStruct((count, near.shape[2]), jnp.bfloat16),
        in_specs=[SMEM, VMEM, VMEM],
        out_specs=VMEM,
        cost_estimate=factor_cost(count, inverse),
        compiler_params=SMALL,
        name="factor_left",
    )(core, near, inverse)


SLOTS = ((0, 4, 2, 6), (1, 5, 3, 7))


def update_kernel(where_ref, active_ref, left_ref, *refs, final):
    if final:
        right_ref, trailing_ref, _, out_ref = refs
        right = right_ref
    else:
        near_ref, far_ref, trailing_ref, out_ref, right = refs
        size = near_ref.shape[0] // 4

        @pl.when(pl.program_id(0) == 0)
        def _():
            for ref, slots in zip((near_ref, far_ref), SLOTS):
                for at, slot in enumerate(slots):
                    block = jnp.bitwise_xor(where_ref[1], slot)
                    right[pl.ds(pl.multiple_of(block * size, size), size), :] = ref[at * size : (at + 1) * size, :]

    x = pl.program_id(0)
    keep = active_ref[x // 2] == 1

    @pl.when(keep)
    def _():
        change = lax.dot_general(
            left_ref[x], right[...], (((1,), (1,)), ((), ())), preferred_element_type=jnp.float32
        )
        out_ref[0, 0] = (trailing_ref[0, 0].astype(jnp.float32) - change).astype(out_ref.dtype)

    @pl.when(jnp.logical_not(keep))
    def _():
        out_ref[0, 0] = trailing_ref[0, 0]


def update(where, active, left, rights, trailing, before=None):
    xs, _, rows, cols = trailing.shape
    features = left.shape[-1]
    picked = pl.BlockSpec((1, 1, rows, cols), lambda x, h, a: (x, h[0], 0, 0))
    final = before is not None
    in_specs = [VMEM] + [VMEM] * len(rights) + [picked]
    operands = [left, *rights, trailing]
    out_shape = [jax.ShapeDtypeStruct(trailing.shape, trailing.dtype)]
    out_specs = [picked]
    aliases = {}
    if final:
        in_specs.append(pl.BlockSpec(memory_space=pl.ANY))
        operands.append(before)
        aliases = {5: 0}
    else:
        out_shape.append(jax.ShapeDtypeStruct((cols, features), jnp.bfloat16))
        out_specs.append(VMEM)
    out = pl.pallas_call(
        functools.partial(update_kernel, final=final),
        out_shape=out_shape,
        grid_spec=pltpu.PrefetchScalarGridSpec(
            num_scalar_prefetch=2,
            grid=(xs,),
            in_specs=in_specs,
            out_specs=out_specs,
        ),
        input_output_aliases=aliases,
        cost_estimate=pl.CostEstimate(
            flops=2 * xs * rows * cols * features,
            bytes_accessed=4 * xs * rows * cols + 2 * cols * features + 2 * left.size,
            transcendentals=0,
        ),
        compiler_params=SMALL,
        name="update_second" if final else "update_first",
    )(where, active, *operands)
    return out


def spread(v, axes, n):
    return lax.all_to_all(jnp.broadcast_to(v[None], (n,) + v.shape), axes, 0, 0)


def swap(v, axis, bit, n):
    return lax.ppermute(v, axis, [(i, i ^ bit) for i in range(n)])


def local(trailing, panel_left, panel_right, inverse_factors, active):
    features = panel_left.shape[1]
    core = lax.axis_index("core").astype(jnp.int32)
    zlo = lax.axis_index("zlo").astype(jnp.int32)
    where = jnp.stack([core, zlo])
    near = spread(panel_left, ("zhi", "core"), 4).reshape(2, -1, features)
    across = swap(panel_right, "zlo", 4, 8)
    pair = factor_right(panel_right, across, inverse_factors)
    again = swap(pair, "zlo", 2, 8)
    quad = jnp.concatenate([pair, again], axis=0)
    far = swap(quad, "zlo", 1, 8)
    left = factor_left(where[:1], near, inverse_factors)
    own = spread(left, ("x", "y"), 32)
    other = swap(own, "core", 1, 2)
    flags = active.reshape(-1)
    view = trailing.reshape(4, 2, trailing.shape[0] // 8, trailing.shape[1])
    first, right = update(where, flags, own.reshape(4, -1, features), (quad, far), view)
    (second,) = update(
        jnp.stack([1 - core, zlo]), flags, other.reshape(4, -1, features), (right,), view, first
    )
    return second.reshape(trailing.shape)


def solution(mesh):
    fine = Mesh(mesh.devices.reshape(8, 4, 2, 8, 2), ("zlo", "x", "zhi", "y", "core"))
    col = ("x", "zhi", "y", "core")
    in_specs = (
        P("zlo", col),
        P(("zlo",) + col, None),
        P(col + ("zlo",), None),
        P(),
        P("zlo", col),
    )
    out_specs = P("zlo", col)
    return jax.shard_map(local, mesh=fine, in_specs=in_specs, out_specs=out_specs, check_vma=False)
```

```python
import jax
import jax.numpy as jnp
from jax import lax
from jax.experimental import pallas as pl
from jax.experimental.pallas import tpu as pltpu
from jax.sharding import Mesh, PartitionSpec as P


VMEM = pl.BlockSpec(memory_space=pltpu.VMEM)
SMEM = pl.BlockSpec(memory_space=pltpu.SMEM)
HBM = pl.BlockSpec(memory_space=pltpu.HBM)
ANY = pl.BlockSpec(memory_space=pl.ANY)
SMALL = pltpu.CompilerParams(vmem_limit_bytes=16 * 2**20)


def in_hbm(array):
    return pltpu.with_memory_space_constraint(array, pltpu.HBM)


def outer_rows(piece, gathered):
    return lax.dot_general(
        piece, gathered, (((1,), (1,)), ((), ())), preferred_element_type=jnp.float32
    )


def copy_all(copies):
    for copy in copies:
        copy.start()
    for copy in copies:
        copy.wait()


def spread_kernel(core_ref, near_ref, spread_hbm, sems):
    peers, few, _ = spread_hbm.shape
    mine = near_ref.at[pl.ds(pl.multiple_of(core_ref[0] * few, few), few)]
    copy_all([pltpu.make_async_copy(mine, spread_hbm.at[peer], sems.at[peer]) for peer in range(peers)])


def spread_rows(core, near, peers):
    return pl.pallas_call(
        spread_kernel,
        out_shape=pltpu.HBM((peers, near.shape[0] // 2, near.shape[1]), near.dtype),
        in_specs=[SMEM, VMEM],
        out_specs=HBM,
        scratch_shapes=[pltpu.SemaphoreType.DMA((peers,))],
        compiler_params=SMALL,
        cost_estimate=pl.CostEstimate(flops=0, bytes_accessed=16 * near.size, transcendentals=0),
        name="spread",
    )(core, near)


def join_kernel(first_any, second_any, out_ref, sems):
    count = first_any.shape[0]
    copy_all(
        [
            pltpu.make_async_copy(ref, out_ref.at[pl.ds(at * count, count)], sems.at[at])
            for at, ref in enumerate((first_any, second_any))
        ]
    )


def join(first, second):
    count, features = first.shape
    return pl.pallas_call(
        join_kernel,
        out_shape=pltpu.VMEM((2 * count, features), first.dtype),
        in_specs=[ANY, ANY],
        out_specs=VMEM,
        scratch_shapes=[pltpu.SemaphoreType.DMA((2,))],
        compiler_params=SMALL,
        cost_estimate=pl.CostEstimate(flops=0, bytes_accessed=8 * first.size, transcendentals=0),
        name="join",
    )(first, second)


def part_columns(at, half):
    return slice(at * half, (2 * at + 1) * half)


def split_kernel(inverse_hbm, parts_ref, inverse_ref, sems):
    panels, width, _ = inverse_hbm.shape
    half = width // 2
    steps = [(panel, at) for panel in range(panels) for at in range(2)]
    copies = []
    for panel, at in steps:
        place = (panel, pl.ds(at * half, half), pl.ds(0, (at + 1) * half))
        copies.append(pltpu.make_async_copy(inverse_hbm.at[place], inverse_ref.at[place], sems.at[panel, at]))
        copies[-1].start()
    for (panel, at), copy in zip(steps, copies):
        copy.wait()
        place = (panel, slice(at * half, (at + 1) * half), slice(0, (at + 1) * half))
        exact = inverse_ref[place]
        high = exact.astype(jnp.bfloat16)
        parts_ref[0, panel, :, part_columns(at, half)] = high
        parts_ref[1, panel, :, part_columns(at, half)] = (exact - high.astype(jnp.float32)).astype(jnp.bfloat16)


def split(inverse):
    panels, width, _ = inverse.shape
    return pl.pallas_call(
        split_kernel,
        out_shape=jax.ShapeDtypeStruct((2, panels, width // 2, 3 * width // 2), jnp.bfloat16),
        in_specs=[HBM],
        out_specs=VMEM,
        scratch_shapes=[pltpu.VMEM(inverse.shape, inverse.dtype), pltpu.SemaphoreType.DMA((inverse.shape[0], 2))],
        compiler_params=SMALL,
        cost_estimate=pl.CostEstimate(flops=4 * inverse.size, bytes_accessed=8 * inverse.size, transcendentals=0),
        name="split",
    )(in_hbm(inverse))


def factor_rows(rows_ref, parts_ref, store):
    _, panels, half, _ = parts_ref.shape
    width = 2 * half
    for panel in range(panels):
        for at in range(2):
            depth = (at + 1) * half
            rows = rows_ref[:, panel * width : panel * width + depth]
            high, rest = (parts_ref[term, panel, :, part_columns(at, half)] for term in range(2))
            total = outer_rows(rows, rest) + outer_rows(rows, high)
            start = panel * width + at * half
            store(slice(start, start + half), total.astype(jnp.bfloat16))


def factor_cost(rows, features, width, copies):
    return pl.CostEstimate(
        flops=4 * rows * features * width,
        bytes_accessed=4 * features * width + 2 * (1 + copies) * rows * features,
        transcendentals=0,
    )


def factor_left_kernel(rows_ref, parts_ref, spread_hbm, done_ref, sems):
    peers, count, _ = spread_hbm.shape
    copies = []

    def store(columns, values):
        done_ref[:, columns] = values
        place = (pl.ds(0, count), pl.ds(columns.start, columns.stop - columns.start))
        step = len(copies) // peers
        for peer in range(peers):
            copies.append(
                pltpu.make_async_copy(done_ref.at[place], spread_hbm.at[(peer,) + place], sems.at[step, peer])
            )
            copies[-1].start()

    factor_rows(rows_ref, parts_ref, store)
    for copy in copies:
        copy.wait()


def factor_left(rows, parts, peers):
    return pl.pallas_call(
        factor_left_kernel,
        out_shape=pltpu.HBM((peers,) + rows.shape, rows.dtype),
        in_specs=[VMEM, VMEM],
        out_specs=HBM,
        scratch_shapes=[pltpu.VMEM(rows.shape, rows.dtype), pltpu.SemaphoreType.DMA((4, peers))],
        compiler_params=SMALL,
        cost_estimate=factor_cost(*rows.shape, 2 * parts.shape[2], peers),
        name="factor_left" if peers > 1 else "factor_right",
    )(rows, parts)


PAIRS = ((0, 4), (2, 6), (1, 5), (3, 7))


def block_starts(zlo_ref, slots, size):
    return [pl.multiple_of(jnp.bitwise_xor(zlo_ref[0], slot) * size, size) for slot in slots]


def gathered_kernel(
    zlo_ref, own_hbm, across_hbm, third_hbm, second_hbm, last_hbm, parts_ref, right_ref, rows_ref, in_sems, out_sems
):
    size = own_hbm.shape[0]
    raw = [
        pltpu.make_async_copy(ref, rows_ref.at[pl.ds(at * size, ref.shape[0])], in_sems.at[at])
        for at, ref in enumerate((own_hbm, across_hbm, third_hbm))
    ]
    placed = []
    for pair, ref in ((1, second_hbm), (3, last_hbm)):
        for at, start in enumerate(block_starts(zlo_ref, PAIRS[pair], size)):
            place = right_ref.at[pl.ds(start, size)]
            placed.append(pltpu.make_async_copy(ref.at[pl.ds(at * size, size)], place, out_sems.at[pair // 2, at]))
    for copy in raw + placed:
        copy.start()
    starts = [start for pair in (0, 2) for start in block_starts(zlo_ref, PAIRS[pair], size)]

    def store(columns, values):
        for at, start in enumerate(starts):
            right_ref[pl.ds(start, size), columns] = values[at * size : (at + 1) * size]

    for copy in raw:
        copy.wait()
    factor_rows(rows_ref, parts_ref, store)
    for copy in placed:
        copy.wait()


def gathered(zlo, own, across, third, second, last, parts):
    size, features = own.shape
    return pl.pallas_call(
        gathered_kernel,
        out_shape=jax.ShapeDtypeStruct((8 * size, features), parts.dtype),
        in_specs=[SMEM, HBM, ANY, ANY, HBM, ANY, VMEM],
        out_specs=VMEM,
        scratch_shapes=[
            pltpu.VMEM((4 * size, features), parts.dtype),
            pltpu.SemaphoreType.DMA((3,)),
            pltpu.SemaphoreType.DMA((2, 2)),
        ],
        compiler_params=SMALL,
        cost_estimate=factor_cost(4 * size, features, 2 * parts.shape[2], 1),
        name="gathered",
    )(zlo, in_hbm(own), across, third, in_hbm(second), last, parts)


def change_tile(tile, tile_rows, active_ref, left_ref, right_ref, trailing_ref, done_ref):
    xs, rows, _ = done_ref.shape
    group = xs // tile_rows
    place = slice(tile * group, (tile + 1) * group)
    left = left_ref[place].reshape(group * rows, left_ref.shape[-1])
    change = outer_rows(left, right_ref[...])
    before = trailing_ref[place].astype(jnp.float32)
    fresh = before - change.reshape(before.shape)
    keep = active_ref[tile] == 1
    done_ref[place] = jnp.where(keep, fresh, before).astype(done_ref.dtype)


def tile_spans(xs, tile_rows):
    group = xs // tile_rows
    return [pl.ds(tile * group, group) for tile in range(tile_rows)]


def first_kernel(half_ref, active_ref, left_any, right_ref, trailing_hbm, done_ref, next_ref, left_ref, trailing_ref, sems):
    half = half_ref[0]
    tile_rows = active_ref.shape[0]
    xs = done_ref.shape[0]
    spans = tile_spans(xs, tile_rows)
    steps = []
    for tile, span in enumerate(spans):
        steps.append(
            (
                pltpu.make_async_copy(left_any.at[span], left_ref.at[span], sems.at[0, tile]),
                pltpu.make_async_copy(trailing_hbm.at[span, half], trailing_ref.at[span], sems.at[1, tile]),
            )
        )
        for copy in steps[-1]:
            copy.start()
    ahead = pltpu.make_async_copy(trailing_hbm.at[pl.ds(0, xs), 1 - half], next_ref, sems.at[2, 0])
    ahead.start()
    for tile, pair in enumerate(steps):
        for copy in pair:
            copy.wait()
        change_tile(tile, tile_rows, active_ref, left_ref, right_ref, trailing_ref, done_ref)
    ahead.wait()


def update_cost(left, right):
    rows = left.shape[0] * left.shape[1]
    return pl.CostEstimate(
        flops=2 * rows * right.size, bytes_accessed=2 * left.size + 2 * right.size + 4 * rows * right.shape[0],
        transcendentals=0,
    )


def update_first(half, active, left, right, trailing):
    shape = left.shape[:2] + trailing.shape[3:]
    return pl.pallas_call(
        first_kernel,
        out_shape=[jax.ShapeDtypeStruct(shape, trailing.dtype)] * 2,
        in_specs=[SMEM] * 2 + [ANY, VMEM, HBM],
        out_specs=[VMEM] * 2,
        scratch_shapes=[
            pltpu.VMEM(left.shape, left.dtype),
            pltpu.VMEM(shape, trailing.dtype),
            pltpu.SemaphoreType.DMA((3, active.shape[0])),
        ],
        compiler_params=SMALL,
        cost_estimate=update_cost(left, right),
        name="update_first",
    )(half, active, left, right, in_hbm(trailing))


def second_kernel(half_ref, active_ref, left_ref, right_ref, first_ref, trailing_ref, out_hbm, done_ref, sems):
    half = half_ref[0]
    tile_rows = active_ref.shape[0]
    xs = first_ref.shape[0]
    copies = [pltpu.make_async_copy(first_ref, out_hbm.at[pl.ds(0, xs), 1 - half], sems.at[tile_rows])]
    copies[0].start()
    for tile, span in enumerate(tile_spans(xs, tile_rows)):
        change_tile(tile, tile_rows, active_ref, left_ref, right_ref, trailing_ref, done_ref)
        copies.append(pltpu.make_async_copy(done_ref.at[span], out_hbm.at[span, half], sems.at[tile]))
        copies[-1].start()
    for copy in copies:
        copy.wait()


def update_second(half, active, left, right, first, held, shape):
    return pl.pallas_call(
        second_kernel,
        out_shape=pltpu.HBM(shape, first.dtype),
        in_specs=[SMEM] * 2 + [VMEM] * 4,
        out_specs=HBM,
        scratch_shapes=[
            pltpu.VMEM(first.shape, first.dtype),
            pltpu.SemaphoreType.DMA((active.shape[0] + 1,)),
        ],
        compiler_params=SMALL,
        cost_estimate=update_cost(left, right),
        name="update_second",
    )(half, active, left, right, first, held)


def swap(v, axis, bit, n):
    return lax.ppermute(v, axis, [(i, i ^ bit) for i in range(n)])


def local(trailing, panel_left, panel_right, inverse_factors, active):
    features = panel_left.shape[1]
    core = lax.axis_index("core").astype(jnp.int32).reshape(1)
    zlo = lax.axis_index("zlo").astype(jnp.int32).reshape(1)
    across = swap(panel_right, "zlo", 4, 8)
    near = lax.all_gather(panel_left, ("zhi", "core"), axis=0, tiled=True)
    spread = spread_rows(core, near, 8)
    pair = join(in_hbm(panel_right), across)
    line = lax.all_to_all(spread, "y", 0, 0).reshape(-1, features)
    parts = split(inverse_factors)
    second = swap(pair, "zlo", 2, 8)
    third = swap(pair, "zlo", 1, 8)
    wide = factor_left(line, parts, 4)
    own = lax.all_to_all(wide, "x", 0, 0)
    second = factor_left(second, parts, 1).reshape(second.shape)
    last = swap(second, "zlo", 1, 8)
    view = trailing.reshape(4, 2, trailing.shape[0] // 8, trailing.shape[1])
    right = gathered(zlo, panel_right, across, third, second, last, parts)
    other = swap(own, "core", 1, 2)
    flags = active.reshape(-1)
    first, held = update_first(core, flags, own, right, view)
    result = update_second(1 - core, flags, other, right, first, held, view.shape)
    return result.reshape(trailing.shape)


def solution(mesh):
    fine = Mesh(mesh.devices.reshape(8, 4, 2, 8, 2), ("zlo", "x", "zhi", "y", "core"))
    col = ("x", "zhi", "y", "core")
    in_specs = (
        P("zlo", col),
        P(("zlo",) + col, None),
        P(col + ("zlo",), None),
        P(),
        P("zlo", col),
    )
    out_specs = P("zlo", col)
    return jax.shard_map(local, mesh=fine, in_specs=in_specs, out_specs=out_specs, check_vma=False)
```

```python
import jax
import jax.numpy as jnp
from jax import lax
from jax.experimental import pallas as pl
from jax.experimental.pallas import tpu as pltpu
from jax.sharding import Mesh, PartitionSpec as P


VMEM = pl.BlockSpec(memory_space=pltpu.VMEM)
SMEM = pl.BlockSpec(memory_space=pltpu.SMEM)
HBM = pl.BlockSpec(memory_space=pltpu.HBM)
ANY = pl.BlockSpec(memory_space=pl.ANY)
SMALL = pltpu.CompilerParams(vmem_limit_bytes=16 * 2**20)


def in_hbm(array):
    return pltpu.with_memory_space_constraint(array, pltpu.HBM)


def outer_rows(piece, gathered):
    return lax.dot_general(
        piece, gathered, (((1,), (1,)), ((), ())), preferred_element_type=jnp.float32
    )


def copy_all(copies):
    for copy in copies:
        copy.start()
    for copy in copies:
        copy.wait()


def spread_kernel(core_ref, near_ref, spread_hbm, sems):
    peers, few, _ = spread_hbm.shape
    mine = near_ref.at[pl.ds(pl.multiple_of(core_ref[0] * few, few), few)]
    copy_all([pltpu.make_async_copy(mine, spread_hbm.at[peer], sems.at[peer]) for peer in range(peers)])


def spread_rows(core, near, peers):
    return pl.pallas_call(
        spread_kernel,
        out_shape=pltpu.HBM((peers, near.shape[0] // 2, near.shape[1]), near.dtype),
        in_specs=[SMEM, VMEM],
        out_specs=HBM,
        scratch_shapes=[pltpu.SemaphoreType.DMA((peers,))],
        compiler_params=SMALL,
        cost_estimate=pl.CostEstimate(flops=0, bytes_accessed=16 * near.size, transcendentals=0),
        name="spread",
    )(core, near)


def join_kernel(first_any, second_any, out_ref, sems):
    count = first_any.shape[0]
    copy_all(
        [
            pltpu.make_async_copy(ref, out_ref.at[pl.ds(at * count, count)], sems.at[at])
            for at, ref in enumerate((first_any, second_any))
        ]
    )


def join(first, second):
    count, features = first.shape
    return pl.pallas_call(
        join_kernel,
        out_shape=pltpu.VMEM((2 * count, features), first.dtype),
        in_specs=[ANY, ANY],
        out_specs=VMEM,
        scratch_shapes=[pltpu.SemaphoreType.DMA((2,))],
        compiler_params=SMALL,
        cost_estimate=pl.CostEstimate(flops=0, bytes_accessed=8 * first.size, transcendentals=0),
        name="join",
    )(first, second)


def part_columns(at, half):
    return slice(at * half, (2 * at + 1) * half)


def split_kernel(inverse_hbm, parts_ref, inverse_ref, sems):
    panels, width, _ = inverse_hbm.shape
    half = width // 2
    steps = [(panel, at) for panel in range(panels) for at in range(2)]
    copies = []
    for panel, at in steps:
        place = (panel, pl.ds(at * half, half), pl.ds(0, (at + 1) * half))
        copies.append(pltpu.make_async_copy(inverse_hbm.at[place], inverse_ref.at[place], sems.at[panel, at]))
        copies[-1].start()
    for (panel, at), copy in zip(steps, copies):
        copy.wait()
        place = (panel, slice(at * half, (at + 1) * half), slice(0, (at + 1) * half))
        exact = inverse_ref[place]
        high = exact.astype(jnp.bfloat16)
        parts_ref[0, panel, :, part_columns(at, half)] = high
        parts_ref[1, panel, :, part_columns(at, half)] = (exact - high.astype(jnp.float32)).astype(jnp.bfloat16)


def split(inverse):
    panels, width, _ = inverse.shape
    return pl.pallas_call(
        split_kernel,
        out_shape=jax.ShapeDtypeStruct((2, panels, width // 2, 3 * width // 2), jnp.bfloat16),
        in_specs=[HBM],
        out_specs=VMEM,
        scratch_shapes=[pltpu.VMEM(inverse.shape, inverse.dtype), pltpu.SemaphoreType.DMA((inverse.shape[0], 2))],
        compiler_params=SMALL,
        cost_estimate=pl.CostEstimate(flops=4 * inverse.size, bytes_accessed=8 * inverse.size, transcendentals=0),
        name="split",
    )(in_hbm(inverse))


def factor_rows(rows_ref, parts_ref, store):
    _, panels, half, _ = parts_ref.shape
    width = 2 * half
    for panel in range(panels):
        for at in range(2):
            depth = (at + 1) * half
            rows = rows_ref[:, panel * width : panel * width + depth]
            high, rest = (parts_ref[term, panel, :, part_columns(at, half)] for term in range(2))
            total = outer_rows(rows, rest) + outer_rows(rows, high)
            start = panel * width + at * half
            store(slice(start, start + half), total.astype(jnp.bfloat16))


def factor_cost(rows, features, width, copies):
    return pl.CostEstimate(
        flops=4 * rows * features * width,
        bytes_accessed=4 * features * width + 2 * (1 + copies) * rows * features,
        transcendentals=0,
    )


def factor_left_kernel(rows_ref, parts_ref, spread_hbm, done_ref, sems):
    peers, count, _ = spread_hbm.shape
    copies = []

    def store(columns, values):
        done_ref[:, columns] = values
        place = (pl.ds(0, count), pl.ds(columns.start, columns.stop - columns.start))
        step = len(copies) // peers
        for peer in range(peers):
            copies.append(
                pltpu.make_async_copy(done_ref.at[place], spread_hbm.at[(peer,) + place], sems.at[step, peer])
            )
            copies[-1].start()

    factor_rows(rows_ref, parts_ref, store)
    for copy in copies:
        copy.wait()


def factor_left(rows, parts, peers):
    return pl.pallas_call(
        factor_left_kernel,
        out_shape=pltpu.HBM((peers,) + rows.shape, rows.dtype),
        in_specs=[VMEM, VMEM],
        out_specs=HBM,
        scratch_shapes=[pltpu.VMEM(rows.shape, rows.dtype), pltpu.SemaphoreType.DMA((4, peers))],
        compiler_params=SMALL,
        cost_estimate=factor_cost(*rows.shape, 2 * parts.shape[2], peers),
        name="factor_left" if peers > 1 else "factor_right",
    )(rows, parts)


PAIRS = ((0, 4), (2, 6), (1, 5), (3, 7))


def block_starts(zlo_ref, slots, size):
    return [pl.multiple_of(jnp.bitwise_xor(zlo_ref[0], slot) * size, size) for slot in slots]


def gathered_kernel(
    zlo_ref, own_hbm, across_hbm, third_hbm, second_hbm, parts_ref, right_ref, rows_ref, in_sems, out_sems
):
    size = own_hbm.shape[0]
    raw = [
        pltpu.make_async_copy(ref, rows_ref.at[pl.ds(at * size, ref.shape[0])], in_sems.at[at])
        for at, ref in enumerate((own_hbm, across_hbm, third_hbm))
    ]
    placed = []
    for at, start in enumerate(block_starts(zlo_ref, PAIRS[1], size)):
        place = right_ref.at[pl.ds(start, size)]
        placed.append(pltpu.make_async_copy(second_hbm.at[pl.ds(at * size, size)], place, out_sems.at[at]))
    for copy in raw + placed:
        copy.start()
    starts = [start for pair in (0, 2) for start in block_starts(zlo_ref, PAIRS[pair], size)]

    def store(columns, values):
        for at, start in enumerate(starts):
            right_ref[pl.ds(start, size), columns] = values[at * size : (at + 1) * size]

    for copy in raw:
        copy.wait()
    factor_rows(rows_ref, parts_ref, store)
    for copy in placed:
        copy.wait()


def gathered(zlo, own, across, third, second, parts):
    size, features = own.shape
    return pl.pallas_call(
        gathered_kernel,
        out_shape=jax.ShapeDtypeStruct((8 * size, features), parts.dtype),
        in_specs=[SMEM, HBM, ANY, ANY, HBM, VMEM],
        out_specs=VMEM,
        scratch_shapes=[
            pltpu.VMEM((4 * size, features), parts.dtype),
            pltpu.SemaphoreType.DMA((3,)),
            pltpu.SemaphoreType.DMA((2,)),
        ],
        compiler_params=SMALL,
        cost_estimate=factor_cost(4 * size, features, 2 * parts.shape[2], 1),
        name="gathered",
    )(zlo, in_hbm(own), across, third, in_hbm(second), parts)


def change_tile(tile, tile_rows, active_ref, left_ref, right_ref, trailing_ref, done_ref):
    xs, rows, _ = done_ref.shape
    group = xs // tile_rows
    place = slice(tile * group, (tile + 1) * group)
    left = left_ref[place].reshape(group * rows, left_ref.shape[-1])
    change = outer_rows(left, right_ref[...])
    before = trailing_ref[place].astype(jnp.float32)
    fresh = before - change.reshape(before.shape)
    keep = active_ref[tile] == 1
    done_ref[place] = jnp.where(keep, fresh, before).astype(done_ref.dtype)


def tile_spans(xs, tile_rows):
    group = xs // tile_rows
    return [pl.ds(tile * group, group) for tile in range(tile_rows)]


def first_kernel(
    half_ref, zlo_ref, active_ref, left_any, right_in, last_any, trailing_hbm, done_ref, next_ref, right_ref,
    left_ref, trailing_ref, sems,
):
    half = half_ref[0]
    tile_rows = active_ref.shape[0]
    xs = done_ref.shape[0]
    size = last_any.shape[0] // 2
    placed = [
        pltpu.make_async_copy(last_any.at[pl.ds(at * size, size)], right_ref.at[pl.ds(start, size)], sems.at[0, at])
        for at, start in enumerate(block_starts(zlo_ref, PAIRS[3], size))
    ]
    arrivals = [
        (
            pltpu.make_async_copy(left_any.at[span], left_ref.at[span], sems.at[3, tile]),
            pltpu.make_async_copy(trailing_hbm.at[span, half], trailing_ref.at[span], sems.at[1, tile]),
        )
        for tile, span in enumerate(tile_spans(xs, tile_rows))
    ]
    ahead = pltpu.make_async_copy(trailing_hbm.at[pl.ds(0, xs), 1 - half], next_ref, sems.at[2, 0])
    for copy in placed + [copy for pair in arrivals for copy in pair] + [ahead]:
        copy.start()
    for copy in placed:
        copy.wait()
    for tile, pair in enumerate(arrivals):
        for copy in pair:
            copy.wait()
        change_tile(tile, tile_rows, active_ref, left_ref, right_ref, trailing_ref, done_ref)
    ahead.wait()


def update_cost(left, right):
    rows = left.shape[0] * left.shape[1]
    return pl.CostEstimate(
        flops=2 * rows * right.size, bytes_accessed=2 * left.size + 2 * right.size + 4 * rows * right.shape[0],
        transcendentals=0,
    )


def update_first(half, zlo, active, left, right, last, trailing):
    shape = left.shape[:2] + trailing.shape[3:]
    return pl.pallas_call(
        first_kernel,
        out_shape=[jax.ShapeDtypeStruct(shape, trailing.dtype)] * 2 + [jax.ShapeDtypeStruct(right.shape, right.dtype)],
        in_specs=[SMEM] * 3 + [ANY, VMEM, ANY, HBM],
        out_specs=[VMEM] * 3,
        scratch_shapes=[
            pltpu.VMEM(left.shape, left.dtype),
            pltpu.VMEM(shape, trailing.dtype),
            pltpu.SemaphoreType.DMA((4, 2)),
        ],
        input_output_aliases={4: 2},
        compiler_params=SMALL,
        cost_estimate=update_cost(left, right),
        name="update_first",
    )(half, zlo, active, left, right, last, in_hbm(trailing))


def second_kernel(half_ref, active_ref, left_ref, right_ref, first_ref, trailing_ref, out_hbm, done_ref, sems):
    half = half_ref[0]
    tile_rows = active_ref.shape[0]
    xs = first_ref.shape[0]
    copies = [pltpu.make_async_copy(first_ref, out_hbm.at[pl.ds(0, xs), 1 - half], sems.at[tile_rows])]
    copies[0].start()
    for tile, span in enumerate(tile_spans(xs, tile_rows)):
        change_tile(tile, tile_rows, active_ref, left_ref, right_ref, trailing_ref, done_ref)
        copies.append(pltpu.make_async_copy(done_ref.at[span], out_hbm.at[span, half], sems.at[tile]))
        copies[-1].start()
    for copy in copies:
        copy.wait()


def update_second(half, active, left, right, first, held, shape):
    return pl.pallas_call(
        second_kernel,
        out_shape=pltpu.HBM(shape, first.dtype),
        in_specs=[SMEM] * 2 + [VMEM] * 4,
        out_specs=HBM,
        scratch_shapes=[
            pltpu.VMEM(first.shape, first.dtype),
            pltpu.SemaphoreType.DMA((active.shape[0] + 1,)),
        ],
        compiler_params=SMALL,
        cost_estimate=update_cost(left, right),
        name="update_second",
    )(half, active, left, right, first, held)


def swap(v, axis, bit, n):
    return lax.ppermute(v, axis, [(i, i ^ bit) for i in range(n)])


def local(trailing, panel_left, panel_right, inverse_factors, active):
    features = panel_left.shape[1]
    core = lax.axis_index("core").astype(jnp.int32).reshape(1)
    zlo = lax.axis_index("zlo").astype(jnp.int32).reshape(1)
    across = swap(panel_right, "zlo", 4, 8)
    near = lax.all_gather(panel_left, ("zhi", "core"), axis=0, tiled=True)
    spread = spread_rows(core, near, 8)
    pair = join(in_hbm(panel_right), across)
    line = lax.all_to_all(spread, "y", 0, 0).reshape(-1, features)
    parts = split(inverse_factors)
    second = swap(pair, "zlo", 2, 8)
    third = swap(pair, "zlo", 1, 8)
    wide = factor_left(line, parts, 4)
    own = lax.all_to_all(wide, "x", 0, 0)
    second = factor_left(second, parts, 1).reshape(second.shape)
    last = swap(second, "zlo", 1, 8)
    view = trailing.reshape(4, 2, trailing.shape[0] // 8, trailing.shape[1])
    right = gathered(zlo, panel_right, across, third, second, parts)
    other = swap(own, "core", 1, 2)
    flags = active.reshape(-1)
    first, held, right = update_first(core, zlo, flags, own, right, last, view)
    result = update_second(1 - core, flags, other, right, first, held, view.shape)
    return result.reshape(trailing.shape)


def solution(mesh):
    fine = Mesh(mesh.devices.reshape(8, 4, 2, 8, 2), ("zlo", "x", "zhi", "y", "core"))
    col = ("x", "zhi", "y", "core")
    in_specs = (
        P("zlo", col),
        P(("zlo",) + col, None),
        P(col + ("zlo",), None),
        P(),
        P("zlo", col),
    )
    out_specs = P("zlo", col)
    return jax.shard_map(local, mesh=fine, in_specs=in_specs, out_specs=out_specs, check_vma=False)
```

```python
import jax
import jax.numpy as jnp
from jax import lax
from jax.experimental import pallas as pl
from jax.experimental.pallas import tpu as pltpu
from jax.sharding import Mesh, PartitionSpec as P


VMEM = pl.BlockSpec(memory_space=pltpu.VMEM)
SMEM = pl.BlockSpec(memory_space=pltpu.SMEM)
HBM = pl.BlockSpec(memory_space=pltpu.HBM)
ANY = pl.BlockSpec(memory_space=pl.ANY)
SMALL = pltpu.CompilerParams(vmem_limit_bytes=16 * 2**20)


def in_hbm(array):
    return pltpu.with_memory_space_constraint(array, pltpu.HBM)


def outer_rows(piece, gathered):
    return lax.dot_general(
        piece, gathered, (((1,), (1,)), ((), ())), preferred_element_type=jnp.float32
    )


def copy_all(copies):
    for copy in copies:
        copy.start()
    for copy in copies:
        copy.wait()


def spread_kernel(core_ref, near_ref, spread_hbm, sems):
    peers, few, _ = spread_hbm.shape
    mine = near_ref.at[pl.ds(pl.multiple_of(core_ref[0] * few, few), few)]
    copy_all([pltpu.make_async_copy(mine, spread_hbm.at[peer], sems.at[peer]) for peer in range(peers)])


def spread_rows(core, near, peers):
    return pl.pallas_call(
        spread_kernel,
        out_shape=pltpu.HBM((peers, near.shape[0] // 2, near.shape[1]), near.dtype),
        in_specs=[SMEM, VMEM],
        out_specs=HBM,
        scratch_shapes=[pltpu.SemaphoreType.DMA((peers,))],
        compiler_params=SMALL,
        cost_estimate=pl.CostEstimate(flops=0, bytes_accessed=16 * near.size, transcendentals=0),
        name="spread",
    )(core, near)


def join_kernel(first_any, second_any, out_ref, sems):
    count = first_any.shape[0]
    copy_all(
        [
            pltpu.make_async_copy(ref, out_ref.at[pl.ds(at * count, count)], sems.at[at])
            for at, ref in enumerate((first_any, second_any))
        ]
    )


def join(first, second):
    count, features = first.shape
    return pl.pallas_call(
        join_kernel,
        out_shape=pltpu.VMEM((2 * count, features), first.dtype),
        in_specs=[ANY, ANY],
        out_specs=VMEM,
        scratch_shapes=[pltpu.SemaphoreType.DMA((2,))],
        compiler_params=SMALL,
        cost_estimate=pl.CostEstimate(flops=0, bytes_accessed=8 * first.size, transcendentals=0),
        name="join",
    )(first, second)


def part_columns(at, half):
    return slice(at * half, (2 * at + 1) * half)


def split_kernel(inverse_hbm, parts_ref, inverse_ref, sems):
    panels, width, _ = inverse_hbm.shape
    half = width // 2
    steps = [(panel, at) for panel in range(panels) for at in range(2)]
    copies = []
    for panel, at in steps:
        place = (panel, pl.ds(at * half, half), pl.ds(0, (at + 1) * half))
        copies.append(pltpu.make_async_copy(inverse_hbm.at[place], inverse_ref.at[place], sems.at[panel, at]))
        copies[-1].start()
    for (panel, at), copy in zip(steps, copies):
        copy.wait()
        place = (panel, slice(at * half, (at + 1) * half), slice(0, (at + 1) * half))
        exact = inverse_ref[place]
        high = exact.astype(jnp.bfloat16)
        parts_ref[0, panel, :, part_columns(at, half)] = high
        parts_ref[1, panel, :, part_columns(at, half)] = (exact - high.astype(jnp.float32)).astype(jnp.bfloat16)


def split(inverse):
    panels, width, _ = inverse.shape
    return pl.pallas_call(
        split_kernel,
        out_shape=jax.ShapeDtypeStruct((2, panels, width // 2, 3 * width // 2), jnp.bfloat16),
        in_specs=[HBM],
        out_specs=VMEM,
        scratch_shapes=[pltpu.VMEM(inverse.shape, inverse.dtype), pltpu.SemaphoreType.DMA((inverse.shape[0], 2))],
        compiler_params=SMALL,
        cost_estimate=pl.CostEstimate(flops=4 * inverse.size, bytes_accessed=8 * inverse.size, transcendentals=0),
        name="split",
    )(in_hbm(inverse))


def factor_rows(rows_ref, parts_ref, store):
    _, panels, half, _ = parts_ref.shape
    width = 2 * half
    for panel in range(panels):
        for at in range(2):
            depth = (at + 1) * half
            rows = rows_ref[:, panel * width : panel * width + depth]
            high, rest = (parts_ref[term, panel, :, part_columns(at, half)] for term in range(2))
            total = outer_rows(rows, rest) + outer_rows(rows, high)
            start = panel * width + at * half
            store(slice(start, start + half), total.astype(jnp.bfloat16))


def factor_cost(rows, features, width, copies):
    return pl.CostEstimate(
        flops=4 * rows * features * width,
        bytes_accessed=4 * features * width + 2 * (1 + copies) * rows * features,
        transcendentals=0,
    )


def factor_left_kernel(rows_ref, parts_ref, spread_hbm, done_ref, sems):
    peers, count, _ = spread_hbm.shape
    copies = []

    def store(columns, values):
        done_ref[:, columns] = values
        place = (pl.ds(0, count), pl.ds(columns.start, columns.stop - columns.start))
        step = len(copies) // peers
        for peer in range(peers):
            copies.append(
                pltpu.make_async_copy(done_ref.at[place], spread_hbm.at[(peer,) + place], sems.at[step, peer])
            )
            copies[-1].start()

    factor_rows(rows_ref, parts_ref, store)
    for copy in copies:
        copy.wait()


def factor_left(rows, parts, peers):
    return pl.pallas_call(
        factor_left_kernel,
        out_shape=pltpu.HBM((peers,) + rows.shape, rows.dtype),
        in_specs=[VMEM, VMEM],
        out_specs=HBM,
        scratch_shapes=[pltpu.VMEM(rows.shape, rows.dtype), pltpu.SemaphoreType.DMA((4, peers))],
        compiler_params=SMALL,
        cost_estimate=factor_cost(*rows.shape, 2 * parts.shape[2], peers),
        name="factor_left" if peers > 1 else "factor_right",
    )(rows, parts)


PAIRS = ((0, 4), (2, 6), (1, 5), (3, 7))


def block_starts(zlo_ref, slots, size):
    return [pl.multiple_of(jnp.bitwise_xor(zlo_ref[0], slot) * size, size) for slot in slots]


def gathered_kernel(
    zlo_ref, half_ref, own_hbm, across_hbm, third_hbm, second_hbm, parts_ref, trailing_hbm, right_ref, held_ref,
    rows_ref, in_sems, out_sems, held_sem,
):
    size = own_hbm.shape[0]
    raw = [
        pltpu.make_async_copy(ref, rows_ref.at[pl.ds(at * size, ref.shape[0])], in_sems.at[at])
        for at, ref in enumerate((own_hbm, across_hbm, third_hbm))
    ]
    placed = []
    for at, start in enumerate(block_starts(zlo_ref, PAIRS[1], size)):
        place = right_ref.at[pl.ds(start, size)]
        placed.append(pltpu.make_async_copy(second_hbm.at[pl.ds(at * size, size)], place, out_sems.at[at]))
    xs = held_ref.shape[0]
    placed.append(pltpu.make_async_copy(trailing_hbm.at[pl.ds(0, xs), half_ref[0]], held_ref, held_sem))
    for copy in raw + placed:
        copy.start()
    starts = [start for pair in (0, 2) for start in block_starts(zlo_ref, PAIRS[pair], size)]

    def store(columns, values):
        for at, start in enumerate(starts):
            right_ref[pl.ds(start, size), columns] = values[at * size : (at + 1) * size]

    for copy in raw:
        copy.wait()
    factor_rows(rows_ref, parts_ref, store)
    for copy in placed:
        copy.wait()


def gathered(zlo, half, own, across, third, second, parts, trailing):
    size, features = own.shape
    xs, _, rows, cols = trailing.shape
    return pl.pallas_call(
        gathered_kernel,
        out_shape=[
            jax.ShapeDtypeStruct((8 * size, features), parts.dtype),
            jax.ShapeDtypeStruct((xs, rows, cols), trailing.dtype),
        ],
        in_specs=[SMEM, SMEM, HBM, ANY, ANY, HBM, VMEM, HBM],
        out_specs=[VMEM] * 2,
        scratch_shapes=[
            pltpu.VMEM((4 * size, features), parts.dtype),
            pltpu.SemaphoreType.DMA((3,)),
            pltpu.SemaphoreType.DMA((2,)),
            pltpu.SemaphoreType.DMA,
        ],
        compiler_params=SMALL,
        cost_estimate=factor_cost(4 * size, features, 2 * parts.shape[2], 1),
        name="gathered",
    )(zlo, half, in_hbm(own), across, third, in_hbm(second), parts, in_hbm(trailing))


def change_tile(tile, tile_rows, active_ref, left_ref, right_ref, trailing_ref, done_ref):
    xs, rows, _ = done_ref.shape
    group = xs // tile_rows
    place = slice(tile * group, (tile + 1) * group)
    left = left_ref[place].reshape(group * rows, left_ref.shape[-1])
    change = outer_rows(left, right_ref[...])
    before = trailing_ref[place].astype(jnp.float32)
    fresh = before - change.reshape(before.shape)
    keep = active_ref[tile] == 1
    done_ref[place] = jnp.where(keep, fresh, before).astype(done_ref.dtype)


def tile_spans(xs, tile_rows):
    group = xs // tile_rows
    return [pl.ds(tile * group, group) for tile in range(tile_rows)]


def first_kernel(
    half_ref, zlo_ref, active_ref, left_any, right_in, last_any, trailing_ref, trailing_hbm, done_ref, next_ref, right_ref,
    left_ref, sems,
):
    tile_rows = active_ref.shape[0]
    size = last_any.shape[0] // 2
    placed = [
        pltpu.make_async_copy(last_any.at[pl.ds(at * size, size)], right_ref.at[pl.ds(start, size)], sems.at[0, at])
        for at, start in enumerate(block_starts(zlo_ref, PAIRS[3], size))
    ]
    arrivals = [
        pltpu.make_async_copy(left_any.at[span], left_ref.at[span], sems.at[1, tile])
        for tile, span in enumerate(tile_spans(done_ref.shape[0], tile_rows))
    ]
    ahead = pltpu.make_async_copy(trailing_hbm.at[pl.ds(0, done_ref.shape[0]), 1 - half_ref[0]], next_ref, sems.at[2, 0])
    for copy in placed + arrivals + [ahead]:
        copy.start()
    for copy in placed:
        copy.wait()
    for tile, copy in enumerate(arrivals):
        copy.wait()
        change_tile(tile, tile_rows, active_ref, left_ref, right_ref, trailing_ref, done_ref)
    ahead.wait()


def update_cost(left, right):
    rows = left.shape[0] * left.shape[1]
    return pl.CostEstimate(
        flops=2 * rows * right.size, bytes_accessed=2 * left.size + 2 * right.size + 4 * rows * right.shape[0],
        transcendentals=0,
    )


def update_first(half, zlo, active, left, right, last, held, trailing):
    return pl.pallas_call(
        first_kernel,
        out_shape=[jax.ShapeDtypeStruct(held.shape, held.dtype)] * 2
        + [jax.ShapeDtypeStruct(right.shape, right.dtype)],
        in_specs=[SMEM] * 3 + [ANY, VMEM, ANY, VMEM, HBM],
        out_specs=[VMEM] * 3,
        scratch_shapes=[pltpu.VMEM(left.shape, left.dtype), pltpu.SemaphoreType.DMA((3, 2))],
        input_output_aliases={4: 2},
        compiler_params=SMALL,
        cost_estimate=update_cost(left, right),
        name="update_first",
    )(half, zlo, active, left, right, last, held, in_hbm(trailing))


def second_kernel(half_ref, active_ref, left_ref, right_ref, first_ref, trailing_ref, out_hbm, done_ref, sems):
    half = half_ref[0]
    tile_rows = active_ref.shape[0]
    xs = first_ref.shape[0]
    copies = [pltpu.make_async_copy(first_ref, out_hbm.at[pl.ds(0, xs), 1 - half], sems.at[tile_rows])]
    copies[0].start()
    for tile, span in enumerate(tile_spans(xs, tile_rows)):
        change_tile(tile, tile_rows, active_ref, left_ref, right_ref, trailing_ref, done_ref)
        copies.append(pltpu.make_async_copy(done_ref.at[span], out_hbm.at[span, half], sems.at[tile]))
        copies[-1].start()
    for copy in copies:
        copy.wait()


def update_second(half, active, left, right, first, held, shape):
    return pl.pallas_call(
        second_kernel,
        out_shape=pltpu.HBM(shape, first.dtype),
        in_specs=[SMEM] * 2 + [VMEM] * 4,
        out_specs=HBM,
        scratch_shapes=[
            pltpu.VMEM(first.shape, first.dtype),
            pltpu.SemaphoreType.DMA((active.shape[0] + 1,)),
        ],
        compiler_params=SMALL,
        cost_estimate=update_cost(left, right),
        name="update_second",
    )(half, active, left, right, first, held)


def swap(v, axis, bit, n):
    return lax.ppermute(v, axis, [(i, i ^ bit) for i in range(n)])


def local(trailing, panel_left, panel_right, inverse_factors, active):
    features = panel_left.shape[1]
    core = lax.axis_index("core").astype(jnp.int32).reshape(1)
    zlo = lax.axis_index("zlo").astype(jnp.int32).reshape(1)
    across = swap(panel_right, "zlo", 4, 8)
    near = lax.all_gather(panel_left, ("zhi", "core"), axis=0, tiled=True)
    spread = spread_rows(core, near, 8)
    pair = join(in_hbm(panel_right), across)
    line = lax.all_to_all(spread, "y", 0, 0).reshape(-1, features)
    parts = split(inverse_factors)
    second = swap(pair, "zlo", 2, 8)
    third = swap(pair, "zlo", 1, 8)
    wide = factor_left(line, parts, 4)
    own = lax.all_to_all(wide, "x", 0, 0)
    second = factor_left(second, parts, 1).reshape(second.shape)
    last = swap(second, "zlo", 1, 8)
    view = trailing.reshape(4, 2, trailing.shape[0] // 8, trailing.shape[1])
    right, held = gathered(zlo, core, panel_right, across, third, second, parts, view)
    other = swap(own, "core", 1, 2)
    flags = active.reshape(-1)
    first, ahead, right = update_first(core, zlo, flags, own, right, last, held, view)
    result = update_second(1 - core, flags, other, right, first, ahead, view.shape)
    return result.reshape(trailing.shape)


def solution(mesh):
    fine = Mesh(mesh.devices.reshape(8, 4, 2, 8, 2), ("zlo", "x", "zhi", "y", "core"))
    col = ("x", "zhi", "y", "core")
    in_specs = (
        P("zlo", col),
        P(("zlo",) + col, None),
        P(col + ("zlo",), None),
        P(),
        P("zlo", col),
    )
    out_specs = P("zlo", col)
    return jax.shard_map(local, mesh=fine, in_specs=in_specs, out_specs=out_specs, check_vma=False)
```
